32 devices in a mesh: groups: 2 (over x), freq: 16 (over z, y, core).
Axes of the slice: x: 2, y: 2, z: 4, core: 2. Of those that a mesh axis runs over, the one named last changes fastest.
Arguments:
- dyson: bfloat16 [128, 4, 2, 512, 512], P(('groups', 'freq')), parts along dimension 0, may hold values from -2.1 to 2.1
- guess: bfloat16 [128, 4, 2, 512, 512], P(('groups', 'freq')), parts along dimension 0, may hold values from -2 to 2
- coulomb: bfloat16 [1024, 512], P('groups'), parts along dimension 0, may hold values from -3 to 3
- partner: int32 [4], replicated, may hold values from 0 to 3, as said below
- freq_index: int32 [2, 64], replicated, may hold values from -128 to 127
Outputs:
- screened: bfloat16 [128, 4, 2, 512, 512], P(('groups', 'freq')), parts along dimension 0
The draws below stay inside these ranges and needn't reach their ends.
There are 2 independent parts, one for each index of `groups`. The reference program is written for one: setup_inputs(seed, part) draws one part's arguments, and reference() takes and returns one part's arrays. A program takes and returns all parts, laid end to end along the dimension named above; an argument that names none is the same for every part. Nothing has to cross between parts.
Inputs may be any that keep to these rules, and one draw needn't show every extreme that they name: partner is a permutation of the 4 lattice vectors.
All inputs are finite; a program needn't handle non-finite values.
Results may differ from the reference program's by a relative error of at most 0.0069.
Values may be sent and summed in bfloat16 or wider, within the bound.
A program may use at most 256 MiB of HBM per device.

```python
import math
import jax
import jax.numpy as jnp
from jax import lax

M = 512
NW = 64
NT = 64
NR = 4


def common_fields(key):
    bit_count = M.bit_length() - 1
    angles = jax.random.uniform(jax.random.fold_in(key, 31), (NR, bit_count), minval=0.3, maxval=1.27)
    indices = jnp.arange(M)
    ortho = jnp.ones((NR, M, M), jnp.float32)
    for level in range(bit_count):
        bit_value = indices // 2 ** level % 2
        same_bit = (bit_value[:, None] == bit_value[None, :])[None]
        lower_bit = (bit_value[:, None] < bit_value[None, :])[None]
        cosine = jnp.cos(angles[:, level])[:, None, None]
        sine_part = jnp.sin(angles[:, level])[:, None, None]
        ortho = ortho * jnp.where(same_bit, cosine, jnp.where(lower_bit, sine_part, -sine_part))
    magnitude = jnp.exp(jax.random.uniform(jax.random.fold_in(key, 32), (NW, NR, M), minval=math.log(0.5), maxval=math.log(2.0)))
    phases = jax.random.uniform(jax.random.fold_in(key, 33), (NW, NR, M), minval=-math.pi, maxval=math.pi)
    return (ortho, magnitude, phases)


def draw_dyson(key, part):
    ortho, magnitude, phases = common_fields(key)
    noise_scale = 0.15 / math.sqrt(M)
    noise = jnp.clip(jax.random.normal(jax.random.fold_in(key, 34), (NW, NR, 2, M, M)), -6.0, 6.0) * noise_scale
    real_part = ortho[None] * (magnitude * jnp.cos(phases))[:, :, None, :]
    imag_part = ortho[None] * (magnitude * jnp.sin(phases))[:, :, None, :]
    return (jnp.stack([real_part, imag_part], axis=2) + noise).astype(jnp.bfloat16)


def draw_guess(key, part):
    ortho, magnitude, phases = common_fields(key)
    turned = jnp.swapaxes(ortho, 1, 2)[None]
    real_part = turned * (jnp.cos(phases) / magnitude)[:, :, :, None]
    imag_part = -turned * (jnp.sin(phases) / magnitude)[:, :, :, None]
    return jnp.stack([real_part, imag_part], axis=2).astype(jnp.bfloat16)


def draw_partner(key, part):
    return jax.random.permutation(jax.random.fold_in(key, 21), NR).astype(jnp.int32)


def place_ends(values, stream_key, low, high):
    index_at = [jax.random.randint(jax.random.fold_in(stream_key, axis), (), 0, length) for axis, length in enumerate(values.shape)]
    longest = values.shape.index(max(values.shape))
    next_to = index_at[:longest] + [(index_at[longest] + 1) % values.shape[longest]] + index_at[longest + 1:]
    return values.at[tuple(index_at)].set(low).at[tuple(next_to)].set(high)


def bell_draw(rng, shape, width, bound, kind=jnp.bfloat16):
    values = width * jax.random.normal(rng, shape, jnp.float32)
    return jnp.clip(values, min=-bound, max=bound).astype(kind)


def setup_inputs(seed: int = 0, part: int = 0) -> dict:
    streams_of = jax.random.split(jax.random.key(seed), 6)
    part_splits = jax.random.split(jax.random.fold_in(streams_of[5], part), 6)
    dyson = draw_dyson(jax.random.fold_in(jax.random.fold_in(streams_of[5], part), 71), part)
    guess = draw_guess(jax.random.fold_in(jax.random.fold_in(streams_of[5], part), 71), part)
    coulomb = bell_draw(part_splits[2], (M, M), 0.5, 3.0)
    partner = draw_partner(jax.random.fold_in(streams_of[5], 71), part)
    freq_index = place_ends(jax.random.randint(streams_of[4], (2, NW), -2 * NW, 2 * NW), jax.random.fold_in(streams_of[4], 1), -2 * NW, (2 * NW) - 1).astype(jnp.int32)
    return {"dyson": dyson, "guess": guess, "coulomb": coulomb, "partner": partner, "freq_index": freq_index}


def fermion_table(freq_index, time_count):
    freq_count = freq_index.shape[1]
    odd_freq = 2 * freq_index[0] + 1
    odd_time = 2 * jnp.arange(time_count, dtype=jnp.int32) + 1
    phases = jnp.mod(odd_time[:, None] * odd_freq[None, :], 4 * time_count)
    angles = phases.astype(jnp.float32) * (math.pi / (2 * time_count))
    cosine = jnp.cos(angles) / math.sqrt(freq_count)
    sine_part = jnp.sin(angles) / math.sqrt(freq_count)
    real_rows = jnp.stack([cosine, sine_part], axis=-1)
    imag_rows = jnp.stack([-sine_part, cosine], axis=-1)
    return jnp.stack([real_rows, imag_rows], axis=1).astype(jnp.bfloat16)

def boson_table(freq_index, time_count):
    odd_time = 2 * jnp.arange(time_count, dtype=jnp.int32) + 1
    phases = jnp.mod(freq_index[1][:, None] * odd_time[None, :], 2 * time_count)
    angles = phases.astype(jnp.float32) * (math.pi / time_count)
    cosine = jnp.cos(angles) / math.sqrt(time_count)
    sine_part = jnp.sin(angles) / math.sqrt(time_count)
    real_rows = jnp.stack([cosine, -sine_part], axis=-1)
    imag_rows = jnp.stack([sine_part, cosine], axis=-1)
    return jnp.stack([real_rows, imag_rows], axis=1).astype(jnp.bfloat16)

def matrix_dot(left_matrix, right_matrix):
    return jnp.dot(left_matrix, right_matrix, preferred_element_type=jnp.float32)

def newton_matrix(dyson_one, guess_one):
    dyson_real, dyson_imag = (dyson_one[0], dyson_one[1])
    guess_real, guess_imag = (guess_one[0], guess_one[1])
    product_real = matrix_dot(dyson_real, guess_real) - matrix_dot(dyson_imag, guess_imag)
    product_imag = matrix_dot(dyson_real, guess_imag) + matrix_dot(dyson_imag, guess_real)
    unit_matrix = jnp.eye(dyson_real.shape[0], dtype=jnp.float32)
    corr_real = (2.0 * unit_matrix - product_real).astype(jnp.bfloat16)
    corr_imag = (-product_imag).astype(jnp.bfloat16)
    green_real = matrix_dot(guess_real, corr_real) - matrix_dot(guess_imag, corr_imag)
    green_imag = matrix_dot(guess_real, corr_imag) + matrix_dot(guess_imag, corr_real)
    return jnp.stack([green_real, green_imag]).astype(jnp.bfloat16)

def reference(dyson, guess, coulomb, partner, freq_index):
    forward = fermion_table(freq_index, NT).astype(jnp.float32)
    backward = boson_table(freq_index, NT).astype(jnp.float32)

    def newton_frequency(inputs):
        dyson_freq, guess_freq = inputs
        return jnp.stack([newton_matrix(dyson_freq[vector], guess_freq[vector]) for vector in range(NR)])
    green = lax.map(newton_frequency, (dyson, guess))
    hole = jnp.swapaxes(jnp.take(green, partner, axis=1), -1, -2)

    def polar_vector(inputs):
        green_vec, hole_vec = inputs
        green_time = jnp.einsum('tdwc,wcij->tdij', forward, green_vec.astype(jnp.float32), precision=lax.Precision.HIGHEST)
        hole_time = jnp.einsum('tdwc,wcij->tdij', forward, hole_vec.astype(jnp.float32), precision=lax.Precision.HIGHEST)
        hole_time = hole_time[::-1]
        polar_real = green_time[:, 0] * hole_time[:, 0] - green_time[:, 1] * hole_time[:, 1]
        polar_imag = green_time[:, 0] * hole_time[:, 1] + green_time[:, 1] * hole_time[:, 0]
        polar = jnp.stack([polar_real, polar_imag], axis=1).astype(jnp.bfloat16)
        polar_freq = jnp.einsum('vdtc,tcij->vdij', backward, polar.astype(jnp.float32), precision=lax.Precision.HIGHEST)
        return polar_freq.astype(jnp.bfloat16)
    polar_all = lax.map(polar_vector, (jnp.swapaxes(green, 0, 1), jnp.swapaxes(hole, 0, 1)))
    polar_all = jnp.swapaxes(polar_all, 0, 1)
    coulomb_wide = coulomb.astype(jnp.float32)

    def screen_frequency(polar_freq):
        results = []
        for vector in range(NR):
            vp_real = matrix_dot(coulomb, polar_freq[vector, 0]).astype(jnp.bfloat16)
            vp_imag = matrix_dot(coulomb, polar_freq[vector, 1]).astype(jnp.bfloat16)
            screen_real = coulomb_wide + matrix_dot(vp_real, coulomb)
            screen_imag = matrix_dot(vp_imag, coulomb)
            results.append(jnp.stack([screen_real, screen_imag]))
        return jnp.stack(results).astype(jnp.bfloat16)
    return lax.map(screen_frequency, polar_all)
```

```python
import functools
import math

import jax
import jax.numpy as jnp
from jax import lax
from jax.experimental import pallas as pl
from jax.experimental.pallas import tpu as pltpu
from jax.sharding import PartitionSpec as P

NT = 64


def fermion_table(freq_index, time_count):
    freq_count = freq_index.shape[1]
    odd_freq = 2 * freq_index[0] + 1
    odd_time = 2 * jnp.arange(time_count, dtype=jnp.int32) + 1
    phases = jnp.mod(odd_time[:, None] * odd_freq[None, :], 4 * time_count)
    angles = phases.astype(jnp.float32) * (math.pi / (2 * time_count))
    cosine = jnp.cos(angles) / math.sqrt(freq_count)
    sine_part = jnp.sin(angles) / math.sqrt(freq_count)
    real_rows = jnp.stack([cosine, sine_part], axis=-1)
    imag_rows = jnp.stack([-sine_part, cosine], axis=-1)
    return jnp.stack([real_rows, imag_rows], axis=1).astype(jnp.bfloat16)


def boson_table(freq_index, time_count):
    odd_time = 2 * jnp.arange(time_count, dtype=jnp.int32) + 1
    phases = jnp.mod(freq_index[1][:, None] * odd_time[None, :], 2 * time_count)
    angles = phases.astype(jnp.float32) * (math.pi / time_count)
    cosine = jnp.cos(angles) / math.sqrt(time_count)
    sine_part = jnp.sin(angles) / math.sqrt(time_count)
    real_rows = jnp.stack([cosine, -sine_part], axis=-1)
    imag_rows = jnp.stack([sine_part, cosine], axis=-1)
    return jnp.stack([real_rows, imag_rows], axis=1).astype(jnp.bfloat16)


def batched(left_matrix, right_matrix):
    return jnp.einsum("bij,bjk->bik", left_matrix, right_matrix, preferred_element_type=jnp.float32)


def newton_green(dyson, guess):
    full_shape = dyson.shape
    batch_size = full_shape[0] * full_shape[1]
    matrix_size = full_shape[3]
    flat_dyson = dyson.reshape(batch_size, 2, matrix_size, matrix_size)
    flat_guess = guess.reshape(batch_size, 2, matrix_size, matrix_size)
    dyson_real, dyson_imag = (flat_dyson[:, 0], flat_dyson[:, 1])
    guess_real, guess_imag = (flat_guess[:, 0], flat_guess[:, 1])
    product_real = batched(dyson_real, guess_real) - batched(dyson_imag, guess_imag)
    product_imag = batched(dyson_real, guess_imag) + batched(dyson_imag, guess_real)
    unit_matrix = jnp.eye(matrix_size, dtype=jnp.float32)
    corr_real = (2.0 * unit_matrix - product_real).astype(jnp.bfloat16)
    corr_imag = (-product_imag).astype(jnp.bfloat16)
    green_real = batched(guess_real, corr_real) - batched(guess_imag, corr_imag)
    green_imag = batched(guess_real, corr_imag) + batched(guess_imag, corr_real)
    green_freq = jnp.stack([green_real, green_imag], axis=1).astype(jnp.bfloat16)
    return green_freq.reshape(full_shape)


def to_time(phase_table, values):
    return jnp.einsum("tdwc,wrcse->trdse", phase_table, values, preferred_element_type=jnp.float32)


def to_freq(phase_table, values):
    return jnp.einsum("vdtc,trcse->vrdse", phase_table, values, preferred_element_type=jnp.float32)


def polarize(green_time, hole_time):
    green_real, green_imag = (green_time[:, :, 0], green_time[:, :, 1])
    hole_real, hole_imag = (hole_time[:, :, 0], hole_time[:, :, 1])
    polar_real = green_real * hole_real - green_imag * hole_imag
    polar_imag = green_real * hole_imag + green_imag * hole_real
    return jnp.stack([polar_real, polar_imag], axis=2).astype(jnp.bfloat16)


def screen_block(polar_freq, coulomb):
    screened_polar = jnp.einsum(
        "ij,frcjk->frcik", coulomb, polar_freq, preferred_element_type=jnp.float32
    )
    screened_polar = screened_polar.astype(jnp.bfloat16)
    product = jnp.einsum(
        "frcij,jk->frcik", screened_polar, coulomb, preferred_element_type=jnp.float32
    )
    real_mask = (jnp.arange(2) == 0).astype(jnp.float32)[None, None, :, None, None]
    return (product + real_mask * coulomb.astype(jnp.float32)[None, None, None]).astype(
        jnp.bfloat16
    )


def local(dyson, guess, coulomb, partner, freq_index):
    green_freq = newton_green(dyson, guess)
    forward = fermion_table(freq_index, NT)
    backward = boson_table(freq_index, NT)
    hole_freq = jnp.swapaxes(jnp.take(green_freq, partner, axis=1), 3, 4)
    green_part = lax.all_to_all(green_freq, "freq", split_axis=3, concat_axis=0, tiled=True)
    hole_part = lax.all_to_all(hole_freq, "freq", split_axis=3, concat_axis=0, tiled=True)
    green_time = to_time(forward, green_part)
    hole_time = to_time(forward, hole_part)[::-1]
    polar_freq = to_freq(backward, polarize(green_time, hole_time)).astype(jnp.bfloat16)
    return screen_block(
        lax.all_to_all(polar_freq, "freq", split_axis=0, concat_axis=3, tiled=True), coulomb
    )


MESH = pl.DeviceIdType.MESH
PEERS = 16
TILE = 128
HALF = 64
PAIRS = [(0, 1), (0, 2), (0, 3), (1, 2), (1, 3), (2, 3)]
VMEM_LIMIT = 60 * 2**20


def dot(left, right):
    return jnp.dot(left, right, preferred_element_type=jnp.float32)


def greet_all(me):
    barrier = pltpu.get_barrier_semaphore()
    for step in range(1, PEERS):
        peer = lax.rem(me + step, PEERS)
        pl.semaphore_signal(barrier, inc=1, device_id={"freq": peer}, device_id_type=MESH)
    pl.semaphore_wait(barrier, PEERS - 1)


def green_kernel(freqs, vectors, dyson_ref, guess_ref, recv_ref, corr, green, send, send_sem, recv_sem, own_sem):
    me = lax.axis_index("freq")
    grid_step = pl.program_id(0)
    steps = freqs * vectors
    slot = lax.rem(grid_step, 2)

    def copy_to(step, at_slot, at_step):
        peer = lax.rem(me + step, PEERS)
        return pltpu.make_async_remote_copy(
            src_ref=send.at[at_slot, peer],
            dst_ref=recv_ref.at[me * freqs + at_step // vectors, lax.rem(at_step, vectors)],
            send_sem=send_sem.at[at_slot, step],
            recv_sem=recv_sem.at[me],
            device_id={"freq": peer},
            device_id_type=MESH,
        )

    def copy_own(at_slot, at_step):
        return pltpu.make_async_copy(
            send.at[at_slot, me],
            recv_ref.at[me * freqs + at_step // vectors, lax.rem(at_step, vectors)],
            own_sem.at[at_slot],
        )

    def wait_slot(at_slot, at_step):
        for step in range(1, PEERS):
            copy_to(step, at_slot, at_step).wait_send()
        copy_own(at_slot, at_step).wait()

    @pl.when(grid_step == 0)
    def _():
        greet_all(me)

    size = dyson_ref.shape[-1]
    guess_real, guess_imag = guess_ref[0, 0, 0], guess_ref[0, 0, 1]
    for row in range(0, size, 256):
        rows = pl.ds(row, 256)
        dyson_real, dyson_imag = dyson_ref[0, 0, 0, rows, :], dyson_ref[0, 0, 1, rows, :]
        line = lax.broadcasted_iota(jnp.int32, (256, size), 0) + row
        column = lax.broadcasted_iota(jnp.int32, (256, size), 1)
        twice = jnp.where(line == column, 2.0, 0.0).astype(jnp.float32)
        product_real = dot(dyson_real, guess_real) - dot(dyson_imag, guess_imag)
        product_imag = dot(dyson_real, guess_imag) + dot(dyson_imag, guess_real)
        corr[0, rows, :] = (twice - product_real).astype(jnp.bfloat16)
        corr[1, rows, :] = (-product_imag).astype(jnp.bfloat16)
    corr_real, corr_imag = corr[0], corr[1]
    for row in range(0, size, 256):
        rows = pl.ds(row, 256)
        left_real, left_imag = guess_ref[0, 0, 0, rows, :], guess_ref[0, 0, 1, rows, :]
        green[0, rows, :] = dot(left_real, corr_real) - dot(left_imag, corr_imag)
        green[1, rows, :] = dot(left_real, corr_imag) + dot(left_imag, corr_real)

    @pl.when(grid_step >= 2)
    def _():
        wait_slot(slot, grid_step - 2)

    for part in range(2):
        for index, (low, high) in enumerate(PAIRS):
            upper = green[part, pl.ds(low * TILE, TILE), pl.ds(high * TILE, TILE)].astype(jnp.bfloat16)
            lower = green[part, pl.ds(high * TILE, TILE), pl.ds(low * TILE, TILE)].T.astype(jnp.bfloat16)
            for half in range(2):
                cut = slice(half * HALF, (half + 1) * HALF)
                send[slot, 2 * index + half, part, pl.ds(0, HALF), :] = upper[cut]
                send[slot, 2 * index + half, part, pl.ds(HALF, HALF), :] = lower[cut]
        for block in range(4):
            span = pl.ds(block * TILE, TILE)
            send[slot, 2 * len(PAIRS) + block, part] = green[part, span, span].astype(jnp.bfloat16)

    for step in range(1, PEERS):
        copy_to(step, slot, grid_step).start()
    copy_own(slot, grid_step).start()

    @pl.when(grid_step == steps - 1)
    def _():
        wait_slot((steps - 2) % 2, steps - 2)
        wait_slot((steps - 1) % 2, steps - 1)
        for step in range(1, PEERS):
            peer = lax.rem(me + step, PEERS)
            slab = recv_ref.at[pl.ds(peer * freqs, freqs)]
            pltpu.make_async_remote_copy(
                src_ref=slab,
                dst_ref=slab,
                send_sem=send_sem.at[0, step],
                recv_sem=recv_sem.at[peer],
                device_id={"freq": peer},
                device_id_type=MESH,
            ).wait_recv()


def green_blocks(dyson, guess):
    freqs, vectors, _, size, _ = dyson.shape
    steps = freqs * vectors
    block = pl.BlockSpec((1, 1, 2, size, size), lambda g: (g // vectors, g % vectors, 0, 0, 0))
    return pl.pallas_call(
        functools.partial(green_kernel, freqs, vectors),
        out_shape=jax.ShapeDtypeStruct((freqs * PEERS, vectors, 2, TILE, TILE), jnp.bfloat16),
        grid=(steps,),
        in_specs=[block, block],
        out_specs=pl.BlockSpec(memory_space=pl.ANY),
        scratch_shapes=[
            pltpu.VMEM((2, size, size), jnp.bfloat16),
            pltpu.VMEM((2, size, size), jnp.float32),
            pltpu.VMEM((2, PEERS, 2, TILE, TILE), jnp.bfloat16),
            pltpu.SemaphoreType.DMA((2, PEERS)),
            pltpu.SemaphoreType.DMA((PEERS,)),
            pltpu.SemaphoreType.DMA((2,)),
        ],
        compiler_params=pltpu.CompilerParams(
            collective_id=0, has_side_effects=True, vmem_limit_bytes=VMEM_LIMIT
        ),
    )(dyson, guess)


def exchange_kernel(values_ref, recv_ref, send_sem, recv_sem, own_sem):
    me = lax.axis_index("freq")
    chunk = values_ref.shape[0] // PEERS
    greet_all(me)

    def copy_to(step):
        peer = lax.rem(me + step, PEERS)
        return pltpu.make_async_remote_copy(
            src_ref=values_ref.at[pl.ds(peer * chunk, chunk)],
            dst_ref=recv_ref.at[me],
            send_sem=send_sem.at[step],
            recv_sem=recv_sem.at[step],
            device_id={"freq": peer},
            device_id_type=MESH,
        )

    own = pltpu.make_async_copy(values_ref.at[pl.ds(me * chunk, chunk)], recv_ref.at[me], own_sem)
    for step in range(1, PEERS):
        copy_to(step).start()
    own.start()
    for step in range(1, PEERS):
        copy_to(step).wait_send()
    own.wait()
    for step in range(1, PEERS):
        source = lax.rem(me + PEERS - step, PEERS)
        pltpu.make_async_remote_copy(
            src_ref=recv_ref.at[source],
            dst_ref=recv_ref.at[source],
            send_sem=send_sem.at[step],
            recv_sem=recv_sem.at[step],
            device_id={"freq": source},
            device_id_type=MESH,
        ).wait_recv()


def exchange(values):
    total = values.shape[0]
    return pl.pallas_call(
        exchange_kernel,
        out_shape=jax.ShapeDtypeStruct((PEERS, total // PEERS) + values.shape[1:], values.dtype),
        in_specs=[pl.BlockSpec(memory_space=pl.ANY)],
        out_specs=pl.BlockSpec(memory_space=pl.ANY),
        scratch_shapes=[
            pltpu.SemaphoreType.DMA((PEERS,)),
            pltpu.SemaphoreType.DMA((PEERS,)),
            pltpu.SemaphoreType.DMA,
        ],
        compiler_params=pltpu.CompilerParams(
            collective_id=1, has_side_effects=True, vmem_limit_bytes=VMEM_LIMIT
        ),
    )(values)


def mirror_kernel(diagonal_ref, values_ref, out_ref):
    @pl.when(diagonal_ref[0] == 0)
    def _():
        out_ref[:, :, pl.ds(0, HALF), :] = values_ref[:, :, pl.ds(HALF, HALF), :]
        out_ref[:, :, pl.ds(HALF, HALF), :] = values_ref[:, :, pl.ds(0, HALF), :]

    @pl.when(diagonal_ref[0] != 0)
    def _():
        for row in range(values_ref.shape[0]):
            for part in range(2):
                out_ref[row, part] = values_ref[row, part].astype(jnp.float32).T.astype(jnp.bfloat16)


def mirror(diagonal, values):
    freqs, vectors, _, _, _ = values.shape
    flat = values.reshape(freqs * vectors, 2, TILE, TILE)
    block = pl.BlockSpec((16, 2, TILE, TILE), lambda g, flag: (g, 0, 0, 0))
    out = pl.pallas_call(
        mirror_kernel,
        out_shape=jax.ShapeDtypeStruct(flat.shape, flat.dtype),
        grid_spec=pltpu.PrefetchScalarGridSpec(
            num_scalar_prefetch=1, grid=(flat.shape[0] // 16,), in_specs=[block], out_specs=block
        ),
        compiler_params=pltpu.CompilerParams(vmem_limit_bytes=VMEM_LIMIT),
    )(diagonal, flat)
    return out.reshape(values.shape)


CHUNK = 16
GROUP = 4


def polar_kernel(partner_ref, green_ref, hole_ref, forward_ref, mirrored_ref, backward_ref, out_ref, green_wide, hole_wide, out_wide):
    rows = green_wide.shape[0]
    depth = rows // CHUNK
    green_wide[...] = green_ref[...].reshape(rows, TILE).astype(jnp.float32)
    hole_wide[...] = hole_ref[...].reshape(rows, TILE).astype(jnp.float32)
    times = forward_ref.shape[0] // 2
    for start in range(0, CHUNK, GROUP):
        def gather(wide):
            return jnp.concatenate(
                [wide[pl.ds(start + k, depth, stride=CHUNK), :] for k in range(GROUP)], axis=1
            ).astype(jnp.bfloat16)
        green_time = dot(forward_ref[...], gather(green_wide))
        hole_time = dot(mirrored_ref[...], gather(hole_wide))
        green_real, green_imag = green_time[:times], green_time[times:]
        hole_real, hole_imag = hole_time[:times], hole_time[times:]
        polar_real = green_real * hole_real - green_imag * hole_imag
        polar_imag = green_real * hole_imag + green_imag * hole_real
        polar = jnp.concatenate([polar_real, polar_imag], axis=0).astype(jnp.bfloat16)
        result = dot(backward_ref[...], polar)
        for k in range(GROUP):
            out_wide[pl.ds(start + k, result.shape[0], stride=CHUNK), :] = result[:, k * TILE:(k + 1) * TILE]
    out_ref[...] = out_wide[...].astype(jnp.bfloat16).reshape(out_ref.shape)


def polarization(partner, green, hole, forward, mirrored, backward):
    freqs, vectors, _, _, _ = green.shape
    outs = backward.shape[0] // 2
    table = pl.BlockSpec(forward.shape, lambda r, k, p: (0, 0))
    back_table = pl.BlockSpec(backward.shape, lambda r, k, p: (0, 0))
    return pl.pallas_call(
        polar_kernel,
        out_shape=jax.ShapeDtypeStruct((outs, vectors, 2, TILE, TILE), jnp.bfloat16),
        grid_spec=pltpu.PrefetchScalarGridSpec(
            num_scalar_prefetch=1,
            grid=(vectors, TILE // CHUNK),
            in_specs=[
                pl.BlockSpec((freqs, 1, 2, CHUNK, TILE), lambda r, k, p: (0, r, 0, k, 0)),
                pl.BlockSpec((freqs, 1, 2, CHUNK, TILE), lambda r, k, p: (0, p[r], 0, k, 0)),
                table, table, back_table,
            ],
            out_specs=pl.BlockSpec((outs, 1, 2, CHUNK, TILE), lambda r, k, p: (0, r, 0, k, 0)),
            scratch_shapes=[
                pltpu.VMEM((freqs * 2 * CHUNK, TILE), jnp.float32),
                pltpu.VMEM((freqs * 2 * CHUNK, TILE), jnp.float32),
                pltpu.VMEM((outs * 2 * CHUNK, TILE), jnp.float32),
            ],
        ),
        compiler_params=pltpu.CompilerParams(vmem_limit_bytes=VMEM_LIMIT),
    )(partner, green, hole, forward, mirrored, backward)


def screen_kernel(blocks_ref, coulomb_ref, out_ref, polar, mixed):
    for part in range(2):
        for index, (low, high) in enumerate(PAIRS):
            upper = [blocks_ref[2 * index + half, 0, 0, part, pl.ds(0, HALF), :] for half in range(2)]
            lower = [blocks_ref[2 * index + half, 0, 0, part, pl.ds(HALF, HALF), :] for half in range(2)]
            for half in range(2):
                polar[part, pl.ds(low * TILE + half * HALF, HALF), pl.ds(high * TILE, TILE)] = upper[half]
            turned = jnp.concatenate(lower, axis=0).astype(jnp.float32).T.astype(jnp.bfloat16)
            polar[part, pl.ds(high * TILE, TILE), pl.ds(low * TILE, TILE)] = turned
        for block in range(4):
            span = pl.ds(block * TILE, TILE)
            polar[part, span, span] = blocks_ref[2 * len(PAIRS) + block, 0, 0, part]
    size = coulomb_ref.shape[0]
    for part in range(2):
        for row in range(0, size, 256):
            rows = pl.ds(row, 256)
            mixed[rows, :] = dot(coulomb_ref[rows, :], polar[part]).astype(jnp.bfloat16)
        for row in range(0, size, 256):
            rows = pl.ds(row, 256)
            product = dot(mixed[rows, :], coulomb_ref[...])
            if part == 0:
                product = product + coulomb_ref[rows, :].astype(jnp.float32)
            out_ref[0, 0, part, rows, :] = product.astype(jnp.bfloat16)


def screen_blocks(blocks, coulomb):
    _, freqs, vectors, _, _, _ = blocks.shape
    size = coulomb.shape[0]
    return pl.pallas_call(
        screen_kernel,
        out_shape=jax.ShapeDtypeStruct((freqs, vectors, 2, size, size), jnp.bfloat16),
        grid=(freqs, vectors),
        in_specs=[
            pl.BlockSpec((PEERS, 1, 1, 2, TILE, TILE), lambda v, r: (0, v, r, 0, 0, 0)),
            pl.BlockSpec((size, size), lambda v, r: (0, 0)),
        ],
        out_specs=pl.BlockSpec((1, 1, 2, size, size), lambda v, r: (v, r, 0, 0, 0)),
        scratch_shapes=[
            pltpu.VMEM((2, size, size), jnp.bfloat16),
            pltpu.VMEM((size, size), jnp.bfloat16),
        ],
        compiler_params=pltpu.CompilerParams(vmem_limit_bytes=VMEM_LIMIT),
    )(blocks, coulomb)


def tables(freq_index):
    forward = fermion_table(freq_index, NT)
    backward = boson_table(freq_index, NT)
    freqs = forward.shape[2]
    plain = jnp.transpose(forward, (1, 0, 2, 3)).reshape(2 * NT, 2 * freqs)
    mirrored = jnp.transpose(forward[::-1], (1, 0, 2, 3)).reshape(2 * NT, 2 * freqs)
    back = jnp.transpose(backward, (0, 1, 3, 2)).reshape(2 * freqs, 2 * NT)
    return plain, mirrored, back


def local_paired(dyson, guess, coulomb, partner, freq_index):
    forward, mirrored, backward = tables(freq_index)
    diagonal = (lax.axis_index("freq") >= 2 * len(PAIRS)).astype(jnp.int32).reshape(1)
    green = green_blocks(dyson, guess)
    hole = mirror(diagonal, green)
    polar = polarization(partner, green, hole, forward, mirrored, backward)
    return screen_blocks(exchange(polar), coulomb)


def solution(mesh):
    in_specs = (
        P(("groups", "freq"), None, None, None, None),
        P(("groups", "freq"), None, None, None, None),
        P("groups", None),
        P(),
        P(),
    )
    out_specs = P(("groups", "freq"), None, None, None, None)
    body = local_paired if mesh.shape["freq"] == PEERS else local
    return jax.shard_map(body, mesh=mesh, in_specs=in_specs, out_specs=out_specs, check_vma=False)
```

```python
import functools
import math

import jax
import jax.numpy as jnp
from jax import lax
from jax.experimental import pallas as pl
from jax.experimental.pallas import tpu as pltpu
from jax.sharding import PartitionSpec as P

NT = 64


def fermion_table(freq_index, time_count):
    freq_count = freq_index.shape[1]
    odd_freq = 2 * freq_index[0] + 1
    odd_time = 2 * jnp.arange(time_count, dtype=jnp.int32) + 1
    phases = jnp.mod(odd_time[:, None] * odd_freq[None, :], 4 * time_count)
    angles = phases.astype(jnp.float32) * (math.pi / (2 * time_count))
    cosine = jnp.cos(angles) / math.sqrt(freq_count)
    sine_part = jnp.sin(angles) / math.sqrt(freq_count)
    real_rows = jnp.stack([cosine, sine_part], axis=-1)
    imag_rows = jnp.stack([-sine_part, cosine], axis=-1)
    return jnp.stack([real_rows, imag_rows], axis=1).astype(jnp.bfloat16)


def boson_table(freq_index, time_count):
    odd_time = 2 * jnp.arange(time_count, dtype=jnp.int32) + 1
    phases = jnp.mod(freq_index[1][:, None] * odd_time[None, :], 2 * time_count)
    angles = phases.astype(jnp.float32) * (math.pi / time_count)
    cosine = jnp.cos(angles) / math.sqrt(time_count)
    sine_part = jnp.sin(angles) / math.sqrt(time_count)
    real_rows = jnp.stack([cosine, -sine_part], axis=-1)
    imag_rows = jnp.stack([sine_part, cosine], axis=-1)
    return jnp.stack([real_rows, imag_rows], axis=1).astype(jnp.bfloat16)


def batched(left_matrix, right_matrix):
    return jnp.einsum("bij,bjk->bik", left_matrix, right_matrix, preferred_element_type=jnp.float32)


def newton_green(dyson, guess):
    full_shape = dyson.shape
    batch_size = full_shape[0] * full_shape[1]
    matrix_size = full_shape[3]
    flat_dyson = dyson.reshape(batch_size, 2, matrix_size, matrix_size)
    flat_guess = guess.reshape(batch_size, 2, matrix_size, matrix_size)
    dyson_real, dyson_imag = (flat_dyson[:, 0], flat_dyson[:, 1])
    guess_real, guess_imag = (flat_guess[:, 0], flat_guess[:, 1])
    product_real = batched(dyson_real, guess_real) - batched(dyson_imag, guess_imag)
    product_imag = batched(dyson_real, guess_imag) + batched(dyson_imag, guess_real)
    unit_matrix = jnp.eye(matrix_size, dtype=jnp.float32)
    corr_real = (2.0 * unit_matrix - product_real).astype(jnp.bfloat16)
    corr_imag = (-product_imag).astype(jnp.bfloat16)
    green_real = batched(guess_real, corr_real) - batched(guess_imag, corr_imag)
    green_imag = batched(guess_real, corr_imag) + batched(guess_imag, corr_real)
    green_freq = jnp.stack([green_real, green_imag], axis=1).astype(jnp.bfloat16)
    return green_freq.reshape(full_shape)


def to_time(phase_table, values):
    return jnp.einsum("tdwc,wrcse->trdse", phase_table, values, preferred_element_type=jnp.float32)


def to_freq(phase_table, values):
    return jnp.einsum("vdtc,trcse->vrdse", phase_table, values, preferred_element_type=jnp.float32)


def polarize(green_time, hole_time):
    green_real, green_imag = (green_time[:, :, 0], green_time[:, :, 1])
    hole_real, hole_imag = (hole_time[:, :, 0], hole_time[:, :, 1])
    polar_real = green_real * hole_real - green_imag * hole_imag
    polar_imag = green_real * hole_imag + green_imag * hole_real
    return jnp.stack([polar_real, polar_imag], axis=2).astype(jnp.bfloat16)


def screen_block(polar_freq, coulomb):
    screened_polar = jnp.einsum(
        "ij,frcjk->frcik", coulomb, polar_freq, preferred_element_type=jnp.float32
    )
    screened_polar = screened_polar.astype(jnp.bfloat16)
    product = jnp.einsum(
        "frcij,jk->frcik", screened_polar, coulomb, preferred_element_type=jnp.float32
    )
    real_mask = (jnp.arange(2) == 0).astype(jnp.float32)[None, None, :, None, None]
    return (product + real_mask * coulomb.astype(jnp.float32)[None, None, None]).astype(
        jnp.bfloat16
    )


def local(dyson, guess, coulomb, partner, freq_index):
    green_freq = newton_green(dyson, guess)
    forward = fermion_table(freq_index, NT)
    backward = boson_table(freq_index, NT)
    hole_freq = jnp.swapaxes(jnp.take(green_freq, partner, axis=1), 3, 4)
    green_part = lax.all_to_all(green_freq, "freq", split_axis=3, concat_axis=0, tiled=True)
    hole_part = lax.all_to_all(hole_freq, "freq", split_axis=3, concat_axis=0, tiled=True)
    green_time = to_time(forward, green_part)
    hole_time = to_time(forward, hole_part)[::-1]
    polar_freq = to_freq(backward, polarize(green_time, hole_time)).astype(jnp.bfloat16)
    return screen_block(
        lax.all_to_all(polar_freq, "freq", split_axis=0, concat_axis=3, tiled=True), coulomb
    )


MESH = pl.DeviceIdType.MESH
PEERS = 16
TILE = 128
HALF = 64
PAIRS = [(0, 1), (0, 2), (0, 3), (1, 2), (1, 3), (2, 3)]
VMEM_LIMIT = 60 * 2**20


def dot(left, right):
    return jnp.dot(left, right, preferred_element_type=jnp.float32)


def greet_all(me):
    barrier = pltpu.get_barrier_semaphore()
    for step in range(1, PEERS):
        peer = lax.rem(me + step, PEERS)
        pl.semaphore_signal(barrier, inc=1, device_id={"freq": peer}, device_id_type=MESH)
    pl.semaphore_wait(barrier, PEERS - 1)


def peer_at(me, step):
    half = PEERS // 2
    side = me // half
    if step < half:
        return (1 - side) * half + lax.rem(me + step, half)
    return side * half + lax.rem(me + step - half + 1, half)


def green_kernel(freqs, vectors, dyson_ref, guess_ref, recv_ref, corr, green, send, send_sem, recv_sem, own_sem):
    me = lax.axis_index("freq")
    grid_step = pl.program_id(0)
    steps = freqs * vectors
    freq, vector = grid_step // vectors, lax.rem(grid_step, vectors)

    def remote(step, source, target):
        return pltpu.make_async_remote_copy(
            src_ref=source,
            dst_ref=target,
            send_sem=send_sem.at[step],
            recv_sem=recv_sem.at[me],
            device_id={"freq": peer_at(me, step)},
            device_id_type=MESH,
        )

    @pl.when(grid_step == 0)
    def _():
        greet_all(me)

    size = dyson_ref.shape[-1]
    guess_real, guess_imag = guess_ref[0, 0, 0], guess_ref[0, 0, 1]
    for row in range(0, size, 256):
        rows = pl.ds(row, 256)
        dyson_real, dyson_imag = dyson_ref[0, 0, 0, rows, :], dyson_ref[0, 0, 1, rows, :]
        line = lax.broadcasted_iota(jnp.int32, (256, size), 0) + row
        column = lax.broadcasted_iota(jnp.int32, (256, size), 1)
        twice = jnp.where(line == column, 2.0, 0.0).astype(jnp.float32)
        product_real = dot(dyson_real, guess_real) - dot(dyson_imag, guess_imag)
        product_imag = dot(dyson_real, guess_imag) + dot(dyson_imag, guess_real)
        corr[0, rows, :] = (twice - product_real).astype(jnp.bfloat16)
        corr[1, rows, :] = (-product_imag).astype(jnp.bfloat16)
    corr_real, corr_imag = corr[0], corr[1]
    for row in range(0, size, 256):
        rows = pl.ds(row, 256)
        left_real, left_imag = guess_ref[0, 0, 0, rows, :], guess_ref[0, 0, 1, rows, :]
        green[0, rows, :] = dot(left_real, corr_real) - dot(left_imag, corr_imag)
        green[1, rows, :] = dot(left_real, corr_imag) + dot(left_imag, corr_real)

    for part in range(2):
        for index, (low, high) in enumerate(PAIRS):
            upper = green[part, pl.ds(low * TILE, TILE), pl.ds(high * TILE, TILE)].astype(jnp.bfloat16)
            lower = green[part, pl.ds(high * TILE, TILE), pl.ds(low * TILE, TILE)].T.astype(jnp.bfloat16)
            for half in range(2):
                cut = slice(half * HALF, (half + 1) * HALF)
                send[freq, vector, 2 * index + half, part, pl.ds(0, HALF), :] = upper[cut]
                send[freq, vector, 2 * index + half, part, pl.ds(HALF, HALF), :] = lower[cut]
        for block in range(4):
            span = pl.ds(block * TILE, TILE)
            send[freq, vector, 2 * len(PAIRS) + block, part] = green[part, span, span].astype(jnp.bfloat16)

    for step in range(PEERS - 1):
        remote(step, send.at[freq, vector, peer_at(me, step)], recv_ref.at[me * freqs + freq, vector]).start()
    pltpu.make_async_copy(send.at[freq, vector, me], recv_ref.at[me * freqs + freq, vector], own_sem).start()

    @pl.when(grid_step == steps - 1)
    def _():
        own_slab = recv_ref.at[pl.ds(me * freqs, freqs)]
        for step in range(PEERS - 1):
            remote(step, send.at[:, :, peer_at(me, step)], own_slab).wait_send()
        pltpu.make_async_copy(send.at[:, :, me], own_slab, own_sem).wait()
        for step in range(PEERS - 1):
            peer = peer_at(me, step)
            slab = recv_ref.at[pl.ds(peer * freqs, freqs)]
            pltpu.make_async_remote_copy(
                src_ref=slab,
                dst_ref=slab,
                send_sem=send_sem.at[step],
                recv_sem=recv_sem.at[peer],
                device_id={"freq": peer},
                device_id_type=MESH,
            ).wait_recv()


def green_blocks(dyson, guess):
    freqs, vectors, _, size, _ = dyson.shape
    steps = freqs * vectors
    block = pl.BlockSpec((1, 1, 2, size, size), lambda g: (g // vectors, g % vectors, 0, 0, 0))
    return pl.pallas_call(
        functools.partial(green_kernel, freqs, vectors),
        out_shape=jax.ShapeDtypeStruct((freqs * PEERS, vectors, 2, TILE, TILE), jnp.bfloat16),
        grid=(steps,),
        in_specs=[block, block],
        out_specs=pl.BlockSpec(memory_space=pl.ANY),
        scratch_shapes=[
            pltpu.VMEM((2, size, size), jnp.bfloat16),
            pltpu.VMEM((2, size, size), jnp.float32),
            pltpu.VMEM((freqs, vectors, PEERS, 2, TILE, TILE), jnp.bfloat16),
            pltpu.SemaphoreType.DMA((PEERS - 1,)),
            pltpu.SemaphoreType.DMA((PEERS,)),
            pltpu.SemaphoreType.DMA,
        ],
        compiler_params=pltpu.CompilerParams(
            collective_id=0, has_side_effects=True, vmem_limit_bytes=VMEM_LIMIT
        ),
    )(dyson, guess)


def mirror_kernel(diagonal_ref, values_ref, out_ref):
    @pl.when(diagonal_ref[0] == 0)
    def _():
        out_ref[:, :, pl.ds(0, HALF), :] = values_ref[:, :, pl.ds(HALF, HALF), :]
        out_ref[:, :, pl.ds(HALF, HALF), :] = values_ref[:, :, pl.ds(0, HALF), :]

    @pl.when(diagonal_ref[0] != 0)
    def _():
        for row in range(values_ref.shape[0]):
            for part in range(2):
                out_ref[row, part] = values_ref[row, part].astype(jnp.float32).T.astype(jnp.bfloat16)


def mirror(diagonal, values):
    freqs, vectors, _, _, _ = values.shape
    flat = values.reshape(freqs * vectors, 2, TILE, TILE)
    block = pl.BlockSpec((16, 2, TILE, TILE), lambda g, flag: (g, 0, 0, 0))
    out = pl.pallas_call(
        mirror_kernel,
        out_shape=jax.ShapeDtypeStruct(flat.shape, flat.dtype),
        grid_spec=pltpu.PrefetchScalarGridSpec(
            num_scalar_prefetch=1, grid=(flat.shape[0] // 16,), in_specs=[block], out_specs=block
        ),
        compiler_params=pltpu.CompilerParams(vmem_limit_bytes=VMEM_LIMIT),
    )(diagonal, flat)
    return out.reshape(values.shape)


CHUNK = 16
GROUP = 4


def polar_kernel(
    partner_ref, green_ref, hole_ref, forward_ref, mirrored_ref, backward_ref, recv_ref,
    green_wide, hole_wide, out_wide, send, send_sem, recv_sem, own_sem,
):
    me = lax.axis_index("freq")
    chunk, vector = pl.program_id(0), pl.program_id(1)
    share = send.shape[2] // PEERS

    def remote(step, source, target):
        return pltpu.make_async_remote_copy(
            src_ref=source,
            dst_ref=target,
            send_sem=send_sem.at[step],
            recv_sem=recv_sem.at[me],
            device_id={"freq": peer_at(me, step)},
            device_id_type=MESH,
        )

    @pl.when((chunk == 0) & (vector == 0))
    def _():
        greet_all(me)

    rows = green_wide.shape[0]
    depth = rows // CHUNK
    green_wide[...] = green_ref[...].reshape(rows, TILE).astype(jnp.float32)
    hole_wide[...] = hole_ref[:, partner_ref[vector]].reshape(rows, TILE).astype(jnp.float32)
    times = forward_ref.shape[0] // 2
    for start in range(0, CHUNK, GROUP):
        def gather(wide):
            return jnp.concatenate(
                [wide[pl.ds(start + k, depth, stride=CHUNK), :] for k in range(GROUP)], axis=1
            ).astype(jnp.bfloat16)
        green_time = dot(forward_ref[...], gather(green_wide))
        hole_time = dot(mirrored_ref[...], gather(hole_wide))
        green_real, green_imag = green_time[:times], green_time[times:]
        hole_real, hole_imag = hole_time[:times], hole_time[times:]
        polar_real = green_real * hole_real - green_imag * hole_imag
        polar_imag = green_real * hole_imag + green_imag * hole_real
        polar = jnp.concatenate([polar_real, polar_imag], axis=0).astype(jnp.bfloat16)
        result = dot(backward_ref[...], polar)
        for k in range(GROUP):
            out_wide[pl.ds(start + k, result.shape[0], stride=CHUNK), :] = result[:, k * TILE:(k + 1) * TILE]
    send[chunk, vector] = out_wide[...].astype(jnp.bfloat16).reshape(send.shape[2:])
    for step in range(PEERS - 1):
        part = pl.ds(peer_at(me, step) * share, share)
        remote(step, send.at[chunk, vector, part], recv_ref.at[me, chunk, vector]).start()
    own = pl.ds(me * share, share)
    pltpu.make_async_copy(send.at[chunk, vector, own], recv_ref.at[me, chunk, vector], own_sem).start()

    @pl.when((chunk == pl.num_programs(0) - 1) & (vector == pl.num_programs(1) - 1))
    def _():
        for step in range(PEERS - 1):
            part = pl.ds(peer_at(me, step) * share, share)
            remote(step, send.at[:, :, part], recv_ref.at[me]).wait_send()
        pltpu.make_async_copy(send.at[:, :, own], recv_ref.at[me], own_sem).wait()
        for step in range(PEERS - 1):
            peer = peer_at(me, step)
            pltpu.make_async_remote_copy(
                src_ref=recv_ref.at[peer],
                dst_ref=recv_ref.at[peer],
                send_sem=send_sem.at[step],
                recv_sem=recv_sem.at[peer],
                device_id={"freq": peer},
                device_id_type=MESH,
            ).wait_recv()


def polarization(partner, green, hole, forward, mirrored, backward):
    freqs, vectors, _, _, _ = green.shape
    outs = backward.shape[0] // 2
    chunks = TILE // CHUNK
    return pl.pallas_call(
        polar_kernel,
        out_shape=jax.ShapeDtypeStruct(
            (PEERS, chunks, vectors, outs // PEERS, 2, CHUNK, TILE), jnp.bfloat16
        ),
        grid=(chunks, vectors),
        in_specs=[
            pl.BlockSpec(memory_space=pltpu.SMEM),
            pl.BlockSpec((freqs, 1, 2, CHUNK, TILE), lambda k, r: (0, r, 0, k, 0)),
            pl.BlockSpec((freqs, vectors, 2, CHUNK, TILE), lambda k, r: (0, 0, 0, k, 0)),
            pl.BlockSpec(forward.shape, lambda k, r: (0, 0)),
            pl.BlockSpec(forward.shape, lambda k, r: (0, 0)),
            pl.BlockSpec(backward.shape, lambda k, r: (0, 0)),
        ],
        out_specs=pl.BlockSpec(memory_space=pl.ANY),
        scratch_shapes=[
            pltpu.VMEM((freqs * 2 * CHUNK, TILE), jnp.float32),
            pltpu.VMEM((freqs * 2 * CHUNK, TILE), jnp.float32),
            pltpu.VMEM((outs * 2 * CHUNK, TILE), jnp.float32),
            pltpu.VMEM((chunks, vectors, outs, 2, CHUNK, TILE), jnp.bfloat16),
            pltpu.SemaphoreType.DMA((PEERS - 1,)),
            pltpu.SemaphoreType.DMA((PEERS,)),
            pltpu.SemaphoreType.DMA,
        ],
        compiler_params=pltpu.CompilerParams(
            collective_id=1, has_side_effects=True, vmem_limit_bytes=VMEM_LIMIT
        ),
    )(partner, green, hole, forward, mirrored, backward)


def screen_kernel(blocks_ref, coulomb_ref, out_ref, polar, mixed):
    chunks = blocks_ref.shape[1]
    mid = chunks // 2

    def rows_of(source, part, start, count):
        return blocks_ref[source, pl.ds(start, count), 0, 0, part].reshape(count * CHUNK, TILE)

    for part in range(2):
        for index, (low, high) in enumerate(PAIRS):
            upper = [rows_of(2 * index + half, part, 0, mid) for half in range(2)]
            lower = [rows_of(2 * index + half, part, mid, mid) for half in range(2)]
            for half in range(2):
                polar[part, pl.ds(low * TILE + half * HALF, HALF), pl.ds(high * TILE, TILE)] = upper[half]
            turned = jnp.concatenate(lower, axis=0).astype(jnp.float32).T.astype(jnp.bfloat16)
            polar[part, pl.ds(high * TILE, TILE), pl.ds(low * TILE, TILE)] = turned
        for block in range(4):
            span = pl.ds(block * TILE, TILE)
            polar[part, span, span] = rows_of(2 * len(PAIRS) + block, part, 0, chunks)
    size = coulomb_ref.shape[0]
    for part in range(2):
        for row in range(0, size, 256):
            rows = pl.ds(row, 256)
            mixed[rows, :] = dot(coulomb_ref[rows, :], polar[part]).astype(jnp.bfloat16)
        for row in range(0, size, 256):
            rows = pl.ds(row, 256)
            product = dot(mixed[rows, :], coulomb_ref[...])
            if part == 0:
                product = product + coulomb_ref[rows, :].astype(jnp.float32)
            out_ref[0, 0, part, rows, :] = product.astype(jnp.bfloat16)


def screen_blocks(blocks, coulomb):
    _, chunks, vectors, freqs, _, _, _ = blocks.shape
    size = coulomb.shape[0]
    return pl.pallas_call(
        screen_kernel,
        out_shape=jax.ShapeDtypeStruct((freqs, vectors, 2, size, size), jnp.bfloat16),
        grid=(freqs, vectors),
        in_specs=[
            pl.BlockSpec((PEERS, chunks, 1, 1, 2, CHUNK, TILE), lambda v, r: (0, 0, r, v, 0, 0, 0)),
            pl.BlockSpec((size, size), lambda v, r: (0, 0)),
        ],
        out_specs=pl.BlockSpec((1, 1, 2, size, size), lambda v, r: (v, r, 0, 0, 0)),
        scratch_shapes=[
            pltpu.VMEM((2, size, size), jnp.bfloat16),
            pltpu.VMEM((size, size), jnp.bfloat16),
        ],
        compiler_params=pltpu.CompilerParams(vmem_limit_bytes=VMEM_LIMIT),
    )(blocks, coulomb)


def tables(freq_index):
    forward = fermion_table(freq_index, NT)
    backward = boson_table(freq_index, NT)
    freqs = forward.shape[2]
    plain = jnp.transpose(forward, (1, 0, 2, 3)).reshape(2 * NT, 2 * freqs)
    mirrored = jnp.transpose(forward[::-1], (1, 0, 2, 3)).reshape(2 * NT, 2 * freqs)
    back = jnp.transpose(backward, (0, 1, 3, 2)).reshape(2 * freqs, 2 * NT)
    return plain, mirrored, back


def local_paired(dyson, guess, coulomb, partner, freq_index):
    forward, mirrored, backward = tables(freq_index)
    diagonal = (lax.axis_index("freq") >= 2 * len(PAIRS)).astype(jnp.int32).reshape(1)
    green = green_blocks(dyson, guess)
    hole = mirror(diagonal, green)
    polar = polarization(partner, green, hole, forward, mirrored, backward)
    return screen_blocks(polar, coulomb)


def solution(mesh):
    in_specs = (
        P(("groups", "freq"), None, None, None, None),
        P(("groups", "freq"), None, None, None, None),
        P("groups", None),
        P(),
        P(),
    )
    out_specs = P(("groups", "freq"), None, None, None, None)
    body = local_paired if mesh.shape["freq"] == PEERS else local
    return jax.shard_map(body, mesh=mesh, in_specs=in_specs, out_specs=out_specs, check_vma=False)
```

```python
import functools
import math

import jax
import jax.numpy as jnp
from jax import lax
from jax.experimental import pallas as pl
from jax.experimental.pallas import tpu as pltpu
from jax.sharding import PartitionSpec as P

NT = 64


def fermion_table(freq_index, time_count):
    freq_count = freq_index.shape[1]
    odd_freq = 2 * freq_index[0] + 1
    odd_time = 2 * jnp.arange(time_count, dtype=jnp.int32) + 1
    phases = jnp.mod(odd_time[:, None] * odd_freq[None, :], 4 * time_count)
    angles = phases.astype(jnp.float32) * (math.pi / (2 * time_count))
    cosine = jnp.cos(angles) / math.sqrt(freq_count)
    sine_part = jnp.sin(angles) / math.sqrt(freq_count)
    real_rows = jnp.stack([cosine, sine_part], axis=-1)
    imag_rows = jnp.stack([-sine_part, cosine], axis=-1)
    return jnp.stack([real_rows, imag_rows], axis=1).astype(jnp.bfloat16)


def boson_table(freq_index, time_count):
    odd_time = 2 * jnp.arange(time_count, dtype=jnp.int32) + 1
    phases = jnp.mod(freq_index[1][:, None] * odd_time[None, :], 2 * time_count)
    angles = phases.astype(jnp.float32) * (math.pi / time_count)
    cosine = jnp.cos(angles) / math.sqrt(time_count)
    sine_part = jnp.sin(angles) / math.sqrt(time_count)
    real_rows = jnp.stack([cosine, -sine_part], axis=-1)
    imag_rows = jnp.stack([sine_part, cosine], axis=-1)
    return jnp.stack([real_rows, imag_rows], axis=1).astype(jnp.bfloat16)


def batched(left_matrix, right_matrix):
    return jnp.einsum("bij,bjk->bik", left_matrix, right_matrix, preferred_element_type=jnp.float32)


def newton_green(dyson, guess):
    full_shape = dyson.shape
    batch_size = full_shape[0] * full_shape[1]
    matrix_size = full_shape[3]
    flat_dyson = dyson.reshape(batch_size, 2, matrix_size, matrix_size)
    flat_guess = guess.reshape(batch_size, 2, matrix_size, matrix_size)
    dyson_real, dyson_imag = (flat_dyson[:, 0], flat_dyson[:, 1])
    guess_real, guess_imag = (flat_guess[:, 0], flat_guess[:, 1])
    product_real = batched(dyson_real, guess_real) - batched(dyson_imag, guess_imag)
    product_imag = batched(dyson_real, guess_imag) + batched(dyson_imag, guess_real)
    unit_matrix = jnp.eye(matrix_size, dtype=jnp.float32)
    corr_real = (2.0 * unit_matrix - product_real).astype(jnp.bfloat16)
    corr_imag = (-product_imag).astype(jnp.bfloat16)
    green_real = batched(guess_real, corr_real) - batched(guess_imag, corr_imag)
    green_imag = batched(guess_real, corr_imag) + batched(guess_imag, corr_real)
    green_freq = jnp.stack([green_real, green_imag], axis=1).astype(jnp.bfloat16)
    return green_freq.reshape(full_shape)


def to_time(phase_table, values):
    return jnp.einsum("tdwc,wrcse->trdse", phase_table, values, preferred_element_type=jnp.float32)


def to_freq(phase_table, values):
    return jnp.einsum("vdtc,trcse->vrdse", phase_table, values, preferred_element_type=jnp.float32)


def polarize(green_time, hole_time):
    green_real, green_imag = (green_time[:, :, 0], green_time[:, :, 1])
    hole_real, hole_imag = (hole_time[:, :, 0], hole_time[:, :, 1])
    polar_real = green_real * hole_real - green_imag * hole_imag
    polar_imag = green_real * hole_imag + green_imag * hole_real
    return jnp.stack([polar_real, polar_imag], axis=2).astype(jnp.bfloat16)


def screen_block(polar_freq, coulomb):
    screened_polar = jnp.einsum(
        "ij,frcjk->frcik", coulomb, polar_freq, preferred_element_type=jnp.float32
    )
    screened_polar = screened_polar.astype(jnp.bfloat16)
    product = jnp.einsum(
        "frcij,jk->frcik", screened_polar, coulomb, preferred_element_type=jnp.float32
    )
    real_mask = (jnp.arange(2) == 0).astype(jnp.float32)[None, None, :, None, None]
    return (product + real_mask * coulomb.astype(jnp.float32)[None, None, None]).astype(
        jnp.bfloat16
    )


def local(dyson, guess, coulomb, partner, freq_index):
    green_freq = newton_green(dyson, guess)
    forward = fermion_table(freq_index, NT)
    backward = boson_table(freq_index, NT)
    hole_freq = jnp.swapaxes(jnp.take(green_freq, partner, axis=1), 3, 4)
    green_part = lax.all_to_all(green_freq, "freq", split_axis=3, concat_axis=0, tiled=True)
    hole_part = lax.all_to_all(hole_freq, "freq", split_axis=3, concat_axis=0, tiled=True)
    green_time = to_time(forward, green_part)
    hole_time = to_time(forward, hole_part)[::-1]
    polar_freq = to_freq(backward, polarize(green_time, hole_time)).astype(jnp.bfloat16)
    return screen_block(
        lax.all_to_all(polar_freq, "freq", split_axis=0, concat_axis=3, tiled=True), coulomb
    )


MESH = pl.DeviceIdType.MESH
PEERS = 16
TILE = 128
HALF = 64
PAIRS = [(0, 1), (0, 2), (0, 3), (1, 2), (1, 3), (2, 3)]
VMEM_LIMIT = 60 * 2**20


def dot(left, right):
    return jnp.dot(left, right, preferred_element_type=jnp.float32)


def greet_all(me):
    barrier = pltpu.get_barrier_semaphore()
    for step in range(1, PEERS):
        peer = lax.rem(me + step, PEERS)
        pl.semaphore_signal(barrier, inc=1, device_id={"freq": peer}, device_id_type=MESH)
    pl.semaphore_wait(barrier, PEERS - 1)


def peer_at(me, step):
    half = PEERS // 2
    side = me // half
    if step < half:
        return (1 - side) * half + lax.rem(me + step, half)
    return side * half + lax.rem(me + step - half + 1, half)


def green_kernel(freqs, vectors, dyson_ref, guess_ref, recv_ref, corr, green, send, send_sem, recv_sem, own_sem):
    me = lax.axis_index("freq")
    grid_step = pl.program_id(0)
    steps = freqs * vectors
    freq, vector = grid_step // vectors, lax.rem(grid_step, vectors)

    def remote(step, source, target):
        return pltpu.make_async_remote_copy(
            src_ref=source,
            dst_ref=target,
            send_sem=send_sem.at[step],
            recv_sem=recv_sem.at[me],
            device_id={"freq": peer_at(me, step)},
            device_id_type=MESH,
        )

    @pl.when(grid_step == 0)
    def _():
        greet_all(me)

    size = dyson_ref.shape[-1]
    guess_real, guess_imag = guess_ref[0, 0, 0], guess_ref[0, 0, 1]
    for row in range(0, size, 256):
        rows = pl.ds(row, 256)
        dyson_real, dyson_imag = dyson_ref[0, 0, 0, rows, :], dyson_ref[0, 0, 1, rows, :]
        line = lax.broadcasted_iota(jnp.int32, (256, size), 0) + row
        column = lax.broadcasted_iota(jnp.int32, (256, size), 1)
        twice = jnp.where(line == column, 2.0, 0.0).astype(jnp.float32)
        product_real = dot(dyson_real, guess_real) - dot(dyson_imag, guess_imag)
        product_imag = dot(dyson_real, guess_imag) + dot(dyson_imag, guess_real)
        corr[0, rows, :] = (twice - product_real).astype(jnp.bfloat16)
        corr[1, rows, :] = (-product_imag).astype(jnp.bfloat16)
    corr_real, corr_imag = corr[0], corr[1]
    for row in range(0, size, 256):
        rows = pl.ds(row, 256)
        left_real, left_imag = guess_ref[0, 0, 0, rows, :], guess_ref[0, 0, 1, rows, :]
        green[0, rows, :] = dot(left_real, corr_real) - dot(left_imag, corr_imag)
        green[1, rows, :] = dot(left_real, corr_imag) + dot(left_imag, corr_real)

    for part in range(2):
        for index, (low, high) in enumerate(PAIRS):
            upper = green[part, pl.ds(low * TILE, TILE), pl.ds(high * TILE, TILE)].astype(jnp.bfloat16)
            lower = green[part, pl.ds(high * TILE, TILE), pl.ds(low * TILE, TILE)].T.astype(jnp.bfloat16)
            for half in range(2):
                cut = slice(half * HALF, (half + 1) * HALF)
                send[freq, vector, 2 * index + half, part, pl.ds(0, HALF), :] = upper[cut]
                send[freq, vector, 2 * index + half, part, pl.ds(HALF, HALF), :] = lower[cut]
        for block in range(4):
            span = pl.ds(block * TILE, TILE)
            send[freq, vector, 2 * len(PAIRS) + block, part] = green[part, span, span].astype(jnp.bfloat16)

    for step in range(PEERS - 1):
        remote(step, send.at[freq, vector, peer_at(me, step)], recv_ref.at[me * freqs + freq, vector]).start()
    pltpu.make_async_copy(send.at[freq, vector, me], recv_ref.at[me * freqs + freq, vector], own_sem).start()

    @pl.when(grid_step == steps - 1)
    def _():
        own_slab = recv_ref.at[pl.ds(me * freqs, freqs)]
        for step in range(PEERS - 1):
            remote(step, send.at[:, :, peer_at(me, step)], own_slab).wait_send()
        pltpu.make_async_copy(send.at[:, :, me], own_slab, own_sem).wait()
        for step in range(PEERS - 1):
            peer = peer_at(me, step)
            slab = recv_ref.at[pl.ds(peer * freqs, freqs)]
            pltpu.make_async_remote_copy(
                src_ref=slab,
                dst_ref=slab,
                send_sem=send_sem.at[step],
                recv_sem=recv_sem.at[peer],
                device_id={"freq": peer},
                device_id_type=MESH,
            ).wait_recv()


def green_blocks(dyson, guess):
    freqs, vectors, _, size, _ = dyson.shape
    steps = freqs * vectors
    block = pl.BlockSpec((1, 1, 2, size, size), lambda g: (g // vectors, g % vectors, 0, 0, 0))
    return pl.pallas_call(
        functools.partial(green_kernel, freqs, vectors),
        out_shape=jax.ShapeDtypeStruct((freqs * PEERS, vectors, 2, TILE, TILE), jnp.bfloat16),
        grid=(steps,),
        in_specs=[block, block],
        out_specs=pl.BlockSpec(memory_space=pl.ANY),
        scratch_shapes=[
            pltpu.VMEM((2, size, size), jnp.bfloat16),
            pltpu.VMEM((2, size, size), jnp.float32),
            pltpu.VMEM((freqs, vectors, PEERS, 2, TILE, TILE), jnp.bfloat16),
            pltpu.SemaphoreType.DMA((PEERS - 1,)),
            pltpu.SemaphoreType.DMA((PEERS,)),
            pltpu.SemaphoreType.DMA,
        ],
        compiler_params=pltpu.CompilerParams(
            collective_id=0, has_side_effects=True, vmem_limit_bytes=VMEM_LIMIT
        ),
    )(dyson, guess)


def mirror_kernel(diagonal_ref, values_ref, out_ref):
    @pl.when(diagonal_ref[0] == 0)
    def _():
        out_ref[:, :, pl.ds(0, HALF), :] = values_ref[:, :, pl.ds(HALF, HALF), :]
        out_ref[:, :, pl.ds(HALF, HALF), :] = values_ref[:, :, pl.ds(0, HALF), :]

    @pl.when(diagonal_ref[0] != 0)
    def _():
        for row in range(values_ref.shape[0]):
            for part in range(2):
                out_ref[row, part] = values_ref[row, part].astype(jnp.float32).T.astype(jnp.bfloat16)


def mirror(diagonal, values):
    freqs, vectors, _, _, _ = values.shape
    flat = values.reshape(freqs * vectors, 2, TILE, TILE)
    block = pl.BlockSpec((32, 2, TILE, TILE), lambda g, flag: (g, 0, 0, 0))
    out = pl.pallas_call(
        mirror_kernel,
        out_shape=jax.ShapeDtypeStruct(flat.shape, flat.dtype),
        grid_spec=pltpu.PrefetchScalarGridSpec(
            num_scalar_prefetch=1, grid=(flat.shape[0] // 32,), in_specs=[block], out_specs=block
        ),
        compiler_params=pltpu.CompilerParams(vmem_limit_bytes=VMEM_LIMIT),
    )(diagonal, flat)
    return out.reshape(values.shape)


CHUNK = 16
GROUP = 4


def polar_kernel(
    partner_ref, green_ref, hole_ref, forward_ref, mirrored_ref, backward_ref, recv_ref,
    green_wide, hole_wide, out_wide, send, send_sem, recv_sem, own_sem,
):
    me = lax.axis_index("freq")
    chunk, vector = pl.program_id(0), pl.program_id(1)
    share = send.shape[2] // PEERS

    def remote(step, source, target):
        return pltpu.make_async_remote_copy(
            src_ref=source,
            dst_ref=target,
            send_sem=send_sem.at[step],
            recv_sem=recv_sem.at[me],
            device_id={"freq": peer_at(me, step)},
            device_id_type=MESH,
        )

    @pl.when((chunk == 0) & (vector == 0))
    def _():
        greet_all(me)

    rows = green_wide.shape[0]
    depth = rows // CHUNK
    green_wide[...] = green_ref[...].reshape(rows, TILE).astype(jnp.float32)
    hole_wide[...] = hole_ref[:, partner_ref[vector]].reshape(rows, TILE).astype(jnp.float32)
    times = forward_ref.shape[0] // 2
    for start in range(0, CHUNK, GROUP):
        def gather(wide):
            return jnp.concatenate(
                [wide[pl.ds(start + k, depth, stride=CHUNK), :] for k in range(GROUP)], axis=1
            ).astype(jnp.bfloat16)
        green_time = dot(forward_ref[...], gather(green_wide))
        hole_time = dot(mirrored_ref[...], gather(hole_wide))
        green_real, green_imag = green_time[:times], green_time[times:]
        hole_real, hole_imag = hole_time[:times], hole_time[times:]
        polar_real = green_real * hole_real - green_imag * hole_imag
        polar_imag = green_real * hole_imag + green_imag * hole_real
        polar = jnp.concatenate([polar_real, polar_imag], axis=0).astype(jnp.bfloat16)
        result = dot(backward_ref[...], polar)
        for k in range(GROUP):
            out_wide[pl.ds(start + k, result.shape[0], stride=CHUNK), :] = result[:, k * TILE:(k + 1) * TILE]
    send[chunk, vector] = out_wide[...].astype(jnp.bfloat16).reshape(send.shape[2:])
    for step in range(PEERS - 1):
        part = pl.ds(peer_at(me, step) * share, share)
        remote(step, send.at[chunk, vector, part], recv_ref.at[me, chunk, vector]).start()
    own = pl.ds(me * share, share)
    pltpu.make_async_copy(send.at[chunk, vector, own], recv_ref.at[me, chunk, vector], own_sem).start()

    @pl.when((chunk == pl.num_programs(0) - 1) & (vector == pl.num_programs(1) - 1))
    def _():
        for step in range(PEERS - 1):
            part = pl.ds(peer_at(me, step) * share, share)
            remote(step, send.at[:, :, part], recv_ref.at[me]).wait_send()
        pltpu.make_async_copy(send.at[:, :, own], recv_ref.at[me], own_sem).wait()
        for step in range(PEERS - 1):
            peer = peer_at(me, step)
            pltpu.make_async_remote_copy(
                src_ref=recv_ref.at[peer],
                dst_ref=recv_ref.at[peer],
                send_sem=send_sem.at[step],
                recv_sem=recv_sem.at[peer],
                device_id={"freq": peer},
                device_id_type=MESH,
            ).wait_recv()


def polarization(partner, green, hole, forward, mirrored, backward):
    freqs, vectors, _, _, _ = green.shape
    outs = backward.shape[0] // 2
    chunks = TILE // CHUNK
    return pl.pallas_call(
        polar_kernel,
        out_shape=jax.ShapeDtypeStruct(
            (PEERS, chunks, vectors, outs // PEERS, 2, CHUNK, TILE), jnp.bfloat16
        ),
        grid=(chunks, vectors),
        in_specs=[
            pl.BlockSpec(memory_space=pltpu.SMEM),
            pl.BlockSpec((freqs, 1, 2, CHUNK, TILE), lambda k, r: (0, r, 0, k, 0)),
            pl.BlockSpec((freqs, vectors, 2, CHUNK, TILE), lambda k, r: (0, 0, 0, k, 0)),
            pl.BlockSpec(forward.shape, lambda k, r: (0, 0)),
            pl.BlockSpec(forward.shape, lambda k, r: (0, 0)),
            pl.BlockSpec(backward.shape, lambda k, r: (0, 0)),
        ],
        out_specs=pl.BlockSpec(memory_space=pl.ANY),
        scratch_shapes=[
            pltpu.VMEM((freqs * 2 * CHUNK, TILE), jnp.float32),
            pltpu.VMEM((freqs * 2 * CHUNK, TILE), jnp.float32),
            pltpu.VMEM((outs * 2 * CHUNK, TILE), jnp.float32),
            pltpu.VMEM((chunks, vectors, outs, 2, CHUNK, TILE), jnp.bfloat16),
            pltpu.SemaphoreType.DMA((PEERS - 1,)),
            pltpu.SemaphoreType.DMA((PEERS,)),
            pltpu.SemaphoreType.DMA,
        ],
        compiler_params=pltpu.CompilerParams(
            collective_id=1, has_side_effects=True, vmem_limit_bytes=VMEM_LIMIT
        ),
    )(partner, green, hole, forward, mirrored, backward)


def screen_kernel(blocks_ref, coulomb_ref, out_ref, polar, mixed):
    chunks = blocks_ref.shape[1]
    mid = chunks // 2

    def rows_of(source, part, start, count):
        return blocks_ref[source, pl.ds(start, count), 0, 0, part].reshape(count * CHUNK, TILE)

    for part in range(2):
        for index, (low, high) in enumerate(PAIRS):
            upper = [rows_of(2 * index + half, part, 0, mid) for half in range(2)]
            lower = [rows_of(2 * index + half, part, mid, mid) for half in range(2)]
            for half in range(2):
                polar[part, pl.ds(low * TILE + half * HALF, HALF), pl.ds(high * TILE, TILE)] = upper[half]
            turned = jnp.concatenate(lower, axis=0).astype(jnp.float32).T.astype(jnp.bfloat16)
            polar[part, pl.ds(high * TILE, TILE), pl.ds(low * TILE, TILE)] = turned
        for block in range(4):
            span = pl.ds(block * TILE, TILE)
            polar[part, span, span] = rows_of(2 * len(PAIRS) + block, part, 0, chunks)
    size = coulomb_ref.shape[0]
    for part in range(2):
        for row in range(0, size, 256):
            rows = pl.ds(row, 256)
            mixed[rows, :] = dot(coulomb_ref[rows, :], polar[part]).astype(jnp.bfloat16)
        for row in range(0, size, 256):
            rows = pl.ds(row, 256)
            product = dot(mixed[rows, :], coulomb_ref[...])
            if part == 0:
                product = product + coulomb_ref[rows, :].astype(jnp.float32)
            out_ref[0, 0, part, rows, :] = product.astype(jnp.bfloat16)


def screen_blocks(blocks, coulomb):
    _, chunks, vectors, freqs, _, _, _ = blocks.shape
    size = coulomb.shape[0]
    return pl.pallas_call(
        screen_kernel,
        out_shape=jax.ShapeDtypeStruct((freqs, vectors, 2, size, size), jnp.bfloat16),
        grid=(freqs, vectors),
        in_specs=[
            pl.BlockSpec((PEERS, chunks, 1, 1, 2, CHUNK, TILE), lambda v, r: (0, 0, r, v, 0, 0, 0)),
            pl.BlockSpec((size, size), lambda v, r: (0, 0)),
        ],
        out_specs=pl.BlockSpec((1, 1, 2, size, size), lambda v, r: (v, r, 0, 0, 0)),
        scratch_shapes=[
            pltpu.VMEM((2, size, size), jnp.bfloat16),
            pltpu.VMEM((size, size), jnp.bfloat16),
        ],
        compiler_params=pltpu.CompilerParams(vmem_limit_bytes=VMEM_LIMIT),
    )(blocks, coulomb)


def tables(freq_index):
    forward = fermion_table(freq_index, NT)
    backward = boson_table(freq_index, NT)
    freqs = forward.shape[2]
    plain = jnp.transpose(forward, (1, 0, 2, 3)).reshape(2 * NT, 2 * freqs)
    mirrored = jnp.transpose(forward[::-1], (1, 0, 2, 3)).reshape(2 * NT, 2 * freqs)
    back = jnp.transpose(backward, (0, 1, 3, 2)).reshape(2 * freqs, 2 * NT)
    return plain, mirrored, back


def local_paired(dyson, guess, coulomb, partner, freq_index):
    forward, mirrored, backward = tables(freq_index)
    diagonal = (lax.axis_index("freq") >= 2 * len(PAIRS)).astype(jnp.int32).reshape(1)
    green = green_blocks(dyson, guess)
    hole = mirror(diagonal, green)
    polar = polarization(partner, green, hole, forward, mirrored, backward)
    return screen_blocks(polar, coulomb)


def solution(mesh):
    in_specs = (
        P(("groups", "freq"), None, None, None, None),
        P(("groups", "freq"), None, None, None, None),
        P("groups", None),
        P(),
        P(),
    )
    out_specs = P(("groups", "freq"), None, None, None, None)
    body = local_paired if mesh.shape["freq"] == PEERS else local
    return jax.shard_map(body, mesh=mesh, in_specs=in_specs, out_specs=out_specs, check_vma=False)
```
